32 devices in a mesh: seq: 16 (over z, y, core), fsdp: 2 (over x).
Axes of the slice: x: 2, y: 2, z: 4, core: 2. Of those that a mesh axis runs over, the one named last changes fastest.
Arguments:
- tokens: bfloat16 [2, 2048, 1024], P('fsdp', 'seq'), may hold values from -6 to 6
- qkv_weight: bfloat16 [1, 1024, 3072], P(None, 'fsdp'), may hold values from -1 to 1
- dense_weight: bfloat16 [1, 1024, 1024], P(None, 'fsdp'), may hold values from -0.5 to 0.5
- fc1_weight: bfloat16 [1, 1024, 4096], P(None, 'fsdp'), may hold values from -0.1875 to 0.1875
- fc2_weight: bfloat16 [1, 4096, 1024], P(None, 'fsdp'), may hold values from -0.09375 to 0.09375
- query_bias: bfloat16 [1, 1024], P(None, 'fsdp'), may hold values from -3 to 3
- value_bias: bfloat16 [1, 1024], P(None, 'fsdp'), may hold values from -3 to 3
- dense_bias: bfloat16 [1, 1024], P(None, 'fsdp'), may hold values from -3 to 3
- fc1_bias: bfloat16 [1, 4096], P(None, 'fsdp'), may hold values from -3 to 3
- fc2_bias: bfloat16 [1, 1024], P(None, 'fsdp'), may hold values from -3 to 3
- norm1_gain: bfloat16 [1, 1024], P(None, 'fsdp'), may hold values from 0.099609375 to 1.8984375
- norm1_shift: bfloat16 [1, 1024], P(None, 'fsdp'), may hold values from -3 to 3
- norm2_gain: bfloat16 [1, 1024], P(None, 'fsdp'), may hold values from 0.099609375 to 1.8984375
- norm2_shift: bfloat16 [1, 1024], P(None, 'fsdp'), may hold values from -3 to 3
- out_grad: bfloat16 [2, 2048, 1024], P('fsdp', 'seq'), may hold values from -6 to 6
Outputs:
- result: bfloat16 [2, 2048, 1024], P('fsdp', 'seq')
- input_grad: bfloat16 [2, 2048, 1024], P('fsdp', 'seq')
- qkv_weight_grad: float32 [1, 1024, 3072], P(None, ('seq', 'fsdp'))
- dense_weight_grad: float32 [1, 1024, 1024], P(None, ('seq', 'fsdp'))
- fc1_weight_grad: float32 [1, 1024, 4096], P(None, ('seq', 'fsdp'))
- fc2_weight_grad: float32 [1, 4096, 1024], P(None, ('seq', 'fsdp'))
- query_bias_grad: float32 [1, 1024], P(None, ('seq', 'fsdp'))
- value_bias_grad: float32 [1, 1024], P(None, ('seq', 'fsdp'))
- dense_bias_grad: float32 [1, 1024], P(None, ('seq', 'fsdp'))
- fc1_bias_grad: float32 [1, 4096], P(None, ('seq', 'fsdp'))
- fc2_bias_grad: float32 [1, 1024], P(None, ('seq', 'fsdp'))
- norm1_gain_grad: float32 [1, 1024], P(None, ('seq', 'fsdp'))
- norm1_shift_grad: float32 [1, 1024], P(None, ('seq', 'fsdp'))
- norm2_gain_grad: float32 [1, 1024], P(None, ('seq', 'fsdp'))
- norm2_shift_grad: float32 [1, 1024], P(None, ('seq', 'fsdp'))
The draws below stay inside these ranges and needn't reach their ends.
All inputs are finite; a program needn't handle non-finite values.
Results may differ from the reference program's by a relative error of at most 0.014.
The reference program's roundings to bfloat16 on the way count: a program that leaves them out, or rounds other values in their place, can miss the bound.
Values may be sent and summed in bfloat16 or wider, within the bound.
A program may use at most 256 MiB of HBM per device.

```python
import jax
import jax.numpy as jnp
from jax import lax

D = 1024
HEADS = 16
FF = 4096
LAYERS = 1
LENGTH = 2048
SEQS = 2


def draw_qkv_weight(key, part):
    head_dim = D // HEADS
    base = jax.random.normal(key, (LAYERS, D, HEADS, 3, head_dim), jnp.float32)
    base = jnp.clip(base, -6.0, 6.0) * D ** (-0.5)
    result = base
    return result.reshape(LAYERS, D, 3 * D).astype(jnp.bfloat16)


def raised(values, own_key, source, target, blocks, factor):
    def block_of(position):
        return (jnp.arange(values.shape[position]) // (values.shape[position] // blocks)).reshape((-1,) + (1,) * (values.ndim - 1 - position))

    near = jax.random.permutation(own_key, blocks)[block_of(target)]
    second = (block_of(target) + blocks // 2) % blocks
    return jnp.where((block_of(source) == near) | (block_of(source) == second), factor * values, values)


def steps_of(rng, dims, shards, least, largest):
    loudness = 1.0
    for axis_at, shards_of in shards:
        draws = jax.random.uniform(jax.random.fold_in(jax.random.fold_in(rng, 6), axis_at), (shards_of,), jnp.float32, least / len(shards), largest / len(shards))
        loudness = loudness * jnp.repeat(jnp.exp(draws), dims[axis_at] // shards_of).reshape((-1,) + (1,) * (len(dims) - 1 - axis_at))
    return loudness


def gaussian(rng, shape, scale, most, cuts=(), dtype=jnp.bfloat16):
    drawn = jax.random.normal(rng, shape, jnp.float32) * scale
    if len(cuts) > 0:
        drawn = steps_of(rng, shape, cuts, -0.22, 0.18) * drawn
    return jnp.clip(drawn, min=-most, max=most).astype(dtype)


def bell_draw_with(own_key, extent, spread, most, pieces, heavy, held_as=jnp.bfloat16):
    values = spread * jax.random.normal(own_key, extent, jnp.float32)
    if pieces:
        values = values * steps_of(own_key, extent, pieces, -0.22, 0.18)
    return jnp.clip(raised(values, jax.random.fold_in(own_key, 3), *heavy), -most, most).astype(held_as)


def setup_inputs(seed: int = 0) -> dict:
    keys = jax.random.split(jax.random.key(seed), 16)
    return {
        "tokens": gaussian(keys[0], (SEQS, LENGTH, D), 1.0, 6.0, ((0, 2), (1, 16))),
        "qkv_weight": draw_qkv_weight(jax.random.fold_in(keys[15], 71), 0),
        "dense_weight": gaussian(keys[2], (LAYERS, D, D), (D // 8) ** -0.5, 0.5, ((1, 2),)),
        "fc1_weight": gaussian(keys[3], (LAYERS, D, FF), D ** -0.5, 0.1875, ((1, 2),)),
        "fc2_weight": gaussian(keys[4], (LAYERS, FF, D), FF ** -0.5, 0.09375, ((1, 2),)),
        "query_bias": gaussian(keys[5], (LAYERS, D), 0.5, 3.0, ((1, 2),)),
        "value_bias": gaussian(keys[6], (LAYERS, D), 0.5, 3.0, ((1, 2),)),
        "dense_bias": gaussian(keys[7], (LAYERS, D), 0.5, 3.0, ((1, 2),)),
        "fc1_bias": gaussian(keys[8], (LAYERS, FF), 0.5, 3.0, ((1, 2),)),
        "fc2_bias": gaussian(keys[9], (LAYERS, D), 0.5, 3.0, ((1, 2),)),
        "norm1_gain": jnp.clip(1.0 + 0.18 * jax.random.normal(keys[10], (LAYERS, D), jnp.float32), 0.099609375, 1.8984375).astype(jnp.bfloat16),
        "norm1_shift": gaussian(keys[11], (LAYERS, D), 0.5, 3.0, ((1, 2),)),
        "norm2_gain": jnp.clip(1.0 + 0.18 * jax.random.normal(keys[12], (LAYERS, D), jnp.float32), 0.099609375, 1.8984375).astype(jnp.bfloat16),
        "norm2_shift": gaussian(keys[13], (LAYERS, D), 0.5, 3.0, ((1, 2),)),
        "out_grad": bell_draw_with(keys[14], (SEQS, LENGTH, D), 1.0, 6.0, ((0, 2), (1, 16)), (1, 2, 16, 2.0)),
    }


NORM_EPS = 1e-05
GELU_COEF = 0.7978845608028654
GELU_CUBE = 0.044715

def layer_norm(hidden, gain, shift):
    average = lax.optimization_barrier(jnp.mean(hidden, axis=-1, keepdims=True))
    centred = hidden - average
    inv_std = lax.rsqrt(lax.optimization_barrier(jnp.mean(centred * centred, axis=-1, keepdims=True)) + NORM_EPS)
    normed = centred * inv_std
    return (normed * gain + shift, normed, inv_std)

def norm_back(upstream, normed, inv_std, gain):
    scaled = upstream * gain
    mean_one = lax.optimization_barrier(jnp.mean(scaled, axis=-1, keepdims=True))
    second = lax.optimization_barrier(jnp.mean(scaled * normed, axis=-1, keepdims=True))
    return inv_std * (scaled - mean_one - normed * second)

def gelu_parts(inputs):
    cubed_in = inputs * inputs * inputs
    tangent = jnp.tanh(GELU_COEF * (inputs + GELU_CUBE * cubed_in))
    result = 0.5 * inputs * (1.0 + tangent)
    derivative = 0.5 * (1.0 + tangent) + 0.5 * inputs * (1.0 - tangent * tangent) * GELU_COEF * (1.0 + 3.0 * GELU_CUBE * inputs * inputs)
    return (result, derivative)

def causal_scores(query_rows, key_rows, alibi_slope, start_row, score_scale):
    scores = jnp.dot(query_rows, key_rows.T, preferred_element_type=jnp.float32) * score_scale
    row_pos = start_row + jnp.arange(query_rows.shape[0]).astype(jnp.int32)[:, None]
    col_pos = jnp.arange(key_rows.shape[0]).astype(jnp.int32)[None, :]
    offset = row_pos - col_pos
    return jnp.where(offset >= 0, scores - alibi_slope * offset.astype(jnp.float32), -jnp.inf)

def attend_one(packed, alibi_slope):
    head_dim = packed.shape[1] // 3
    score_scale = head_dim ** (-0.5)
    length_all = packed.shape[0]
    block_rows = min(2048, length_all)
    queries = packed[:, :head_dim]
    key_part = packed[:, head_dim:2 * head_dim]
    values = packed[:, 2 * head_dim:]
    outputs = []
    totals = []
    for start_row in range(0, length_all, block_rows):
        end_row = start_row + block_rows
        scores = causal_scores(queries[start_row:end_row], key_part[:end_row], alibi_slope, start_row, score_scale)
        top_score = lax.optimization_barrier(jnp.max(scores, axis=1, keepdims=True))
        log_total = top_score[:, 0] + jnp.log(lax.optimization_barrier(jnp.sum(jnp.exp(scores - top_score), axis=1)))
        probs = jnp.exp(scores - log_total[:, None]).astype(jnp.bfloat16)
        outputs.append(jnp.dot(probs, values[:end_row], preferred_element_type=jnp.float32).astype(jnp.bfloat16))
        totals.append(log_total)
    return (jnp.concatenate(outputs, axis=0), jnp.concatenate(totals, axis=0))

def attend_back_one(packed, head_out, log_total, grad_out, alibi_slope):
    head_dim = packed.shape[1] // 3
    score_scale = head_dim ** (-0.5)
    length_all = packed.shape[0]
    block_rows = min(2048, length_all)
    queries = packed[:, :head_dim]
    key_part = packed[:, head_dim:2 * head_dim]
    values = packed[:, 2 * head_dim:]
    row_delta = lax.optimization_barrier(jnp.sum(grad_out.astype(jnp.float32) * head_out.astype(jnp.float32), axis=1))
    d_key_total = jnp.zeros((length_all, head_dim), jnp.float32)
    d_value_total = jnp.zeros((length_all, head_dim), jnp.float32)
    d_query_rows = []
    for start_row in range(0, length_all, block_rows):
        end_row = start_row + block_rows
        query_rows = queries[start_row:end_row]
        grad_rows = grad_out[start_row:end_row]
        scores = causal_scores(query_rows, key_part[:end_row], alibi_slope, start_row, score_scale)
        probs = jnp.exp(scores - log_total[start_row:end_row, None])
        probs_low = probs.astype(jnp.bfloat16)
        d_value_total = d_value_total.at[:end_row].add(jnp.dot(probs_low.T, grad_rows, preferred_element_type=jnp.float32))
        d_probs = jnp.dot(grad_rows, values[:end_row].T, preferred_element_type=jnp.float32)
        d_scores = (probs * (d_probs - row_delta[start_row:end_row, None])).astype(jnp.bfloat16)
        d_query_rows.append(jnp.dot(d_scores, key_part[:end_row], preferred_element_type=jnp.float32) * score_scale)
        d_key_total = d_key_total.at[:end_row].add(jnp.dot(d_scores.T, query_rows, preferred_element_type=jnp.float32) * score_scale)
    d_query = jnp.concatenate(d_query_rows, axis=0)
    return jnp.concatenate([d_query, d_key_total, d_value_total], axis=1).astype(jnp.bfloat16)

def run_forward(item):
    return attend_one(item[0], item[1])

def run_backward(item):
    return attend_back_one(item[0], item[1], item[2], item[3], item[4])

def to_heads(flat, seq_count, length_all, last_dim):
    return flat.reshape(seq_count, length_all, HEADS, last_dim).transpose(0, 2, 1, 3).reshape(seq_count * HEADS, length_all, last_dim)

def from_heads(stacked, seq_count, length_all):
    last_dim = stacked.shape[2]
    return stacked.reshape(seq_count, HEADS, length_all, last_dim).transpose(0, 2, 1, 3).reshape(seq_count * length_all, HEADS * last_dim)

def reference(tokens, qkv_weight, dense_weight, fc1_weight, fc2_weight, query_bias, value_bias, dense_bias, fc1_bias, fc2_bias, norm1_gain, norm1_shift, norm2_gain, norm2_shift, out_grad):
    seq_count, length_all, model_width = tokens.shape
    head_dim = model_width // HEADS
    slopes = jnp.exp2(-8.0 * (jnp.arange(HEADS) + 1).astype(jnp.float32) / HEADS)
    slope_all = jnp.tile(slopes, seq_count)
    hidden = tokens.reshape(-1, model_width).astype(jnp.float32)
    stored = []
    for layer_at in range(LAYERS):
        gain_one = norm1_gain[layer_at].astype(jnp.float32)
        gain_two = norm2_gain[layer_at].astype(jnp.float32)
        normed_in, hat_one, inv_one = layer_norm(hidden, gain_one, norm1_shift[layer_at].astype(jnp.float32))
        attn_in = normed_in.astype(jnp.bfloat16)
        zero_part = jnp.zeros((HEADS, head_dim), jnp.float32)
        full_bias = jnp.stack([query_bias[layer_at].astype(jnp.float32).reshape(HEADS, head_dim), zero_part, value_bias[layer_at].astype(jnp.float32).reshape(HEADS, head_dim)], axis=1).reshape(-1)
        packed = (jnp.dot(attn_in, qkv_weight[layer_at], preferred_element_type=jnp.float32) + full_bias).astype(jnp.bfloat16)
        head_rows = to_heads(packed, seq_count, length_all, 3 * head_dim)
        head_out, log_total = lax.map(run_forward, (head_rows, slope_all))
        mixed_out = from_heads(head_out, seq_count, length_all)
        after_attn = hidden + jnp.dot(mixed_out, dense_weight[layer_at], preferred_element_type=jnp.float32) + dense_bias[layer_at].astype(jnp.float32)
        normed_mid, hat_two, inv_two = layer_norm(after_attn, gain_two, norm2_shift[layer_at].astype(jnp.float32))
        mlp_in = normed_mid.astype(jnp.bfloat16)
        pre_act = jnp.dot(mlp_in, fc1_weight[layer_at], preferred_element_type=jnp.float32) + fc1_bias[layer_at].astype(jnp.float32)
        activation, gelu_slope = gelu_parts(pre_act)
        act_low = activation.astype(jnp.bfloat16)
        hidden_next = after_attn + jnp.dot(act_low, fc2_weight[layer_at], preferred_element_type=jnp.float32) + fc2_bias[layer_at].astype(jnp.float32)
        stored.append((attn_in, hat_one, inv_one, gain_one, head_rows, head_out, log_total, mixed_out, hat_two, inv_two, gain_two, mlp_in, gelu_slope, act_low))
        hidden = hidden_next
    result = hidden.astype(jnp.bfloat16).reshape(tokens.shape)
    upstream = out_grad.reshape(-1, model_width).astype(jnp.float32)
    grads = []
    for layer_at in range(LAYERS - 1, -1, -1):
        attn_in, hat_one, inv_one, gain_one, head_rows, head_out, log_total, mixed_out, hat_two, inv_two, gain_two, mlp_in, gelu_slope, act_low = stored[layer_at]
        up_low = upstream.astype(jnp.bfloat16)
        g_fc2_w = jnp.dot(act_low.T, up_low, preferred_element_type=jnp.float32)
        g_fc2_b = lax.optimization_barrier(jnp.sum(upstream, axis=0))
        d_pre = jnp.dot(up_low, fc2_weight[layer_at].T, preferred_element_type=jnp.float32) * gelu_slope
        d_pre_low = d_pre.astype(jnp.bfloat16)
        g_fc1_w = jnp.dot(mlp_in.T, d_pre_low, preferred_element_type=jnp.float32)
        g_fc1_b = lax.optimization_barrier(jnp.sum(d_pre, axis=0))
        d_norm2 = jnp.dot(d_pre_low, fc1_weight[layer_at].T, preferred_element_type=jnp.float32)
        g_gain2 = lax.optimization_barrier(jnp.sum(d_norm2 * hat_two, axis=0))
        g_shift2 = lax.optimization_barrier(jnp.sum(d_norm2, axis=0))
        d_after = upstream + norm_back(d_norm2, hat_two, inv_two, gain_two)
        d_after_low = d_after.astype(jnp.bfloat16)
        g_dense_w = jnp.dot(mixed_out.T, d_after_low, preferred_element_type=jnp.float32)
        g_dense_b = lax.optimization_barrier(jnp.sum(d_after, axis=0))
        d_mixed = jnp.dot(d_after_low, dense_weight[layer_at].T, preferred_element_type=jnp.float32).astype(jnp.bfloat16)
        d_heads = to_heads(d_mixed, seq_count, length_all, head_dim)
        d_packed_heads = lax.map(run_backward, (head_rows, head_out, log_total, d_heads, slope_all))
        d_packed = from_heads(d_packed_heads, seq_count, length_all)
        g_qkv_w = jnp.dot(attn_in.T, d_packed, preferred_element_type=jnp.float32)
        col_sums = lax.optimization_barrier(jnp.sum(d_packed.astype(jnp.float32), axis=0)).reshape(HEADS, 3, head_dim)
        g_query_b = col_sums[:, 0, :].reshape(-1)
        g_value_b = col_sums[:, 2, :].reshape(-1)
        d_norm1 = jnp.dot(d_packed, qkv_weight[layer_at].T, preferred_element_type=jnp.float32)
        g_gain1 = lax.optimization_barrier(jnp.sum(d_norm1 * hat_one, axis=0))
        g_shift1 = lax.optimization_barrier(jnp.sum(d_norm1, axis=0))
        upstream = d_after + norm_back(d_norm1, hat_one, inv_one, gain_one)
        grads.append((g_qkv_w, g_dense_w, g_fc1_w, g_fc2_w, g_query_b, g_value_b, g_dense_b, g_fc1_b, g_fc2_b, g_gain1, g_shift1, g_gain2, g_shift2))
    grads = grads[::-1]
    stacked = [jnp.stack([grads[layer_at][member] for layer_at in range(LAYERS)]) for member in range(13)]
    input_grad = upstream.astype(jnp.bfloat16).reshape(tokens.shape)
    return (result, input_grad, stacked[0], stacked[1], stacked[2], stacked[3], stacked[4], stacked[5], stacked[6], stacked[7], stacked[8], stacked[9], stacked[10], stacked[11], stacked[12])
```

```python
import jax
import jax.numpy as jnp
from jax import lax
from jax.sharding import PartitionSpec as P

HEADS = 16


NORM_EPS = 1e-05
GELU_COEF = 0.7978845608028654
GELU_CUBE = 0.044715


def layer_norm(hidden, gain, shift):
    average = jnp.mean(hidden, axis=-1, keepdims=True)
    centred = hidden - average
    inv_std = lax.rsqrt(jnp.mean(centred * centred, axis=-1, keepdims=True) + NORM_EPS)
    normed = centred * inv_std
    return (normed * gain + shift, normed, inv_std)


def norm_back(upstream, normed, inv_std, gain):
    scaled = upstream * gain
    mean_one = jnp.mean(scaled, axis=-1, keepdims=True)
    second = jnp.mean(scaled * normed, axis=-1, keepdims=True)
    return inv_std * (scaled - mean_one - normed * second)


def gelu_parts(inputs):
    cubed_in = inputs * inputs * inputs
    tangent = jnp.tanh(GELU_COEF * (inputs + GELU_CUBE * cubed_in))
    result = 0.5 * inputs * (1.0 + tangent)
    derivative = 0.5 * (1.0 + tangent) + 0.5 * inputs * (1.0 - tangent * tangent) * GELU_COEF * (
        1.0 + 3.0 * GELU_CUBE * inputs * inputs
    )
    return (result, derivative)


def masked_scores(query_rows, key_rows, row_pos, alibi_slope, score_scale):
    scores = (
        jnp.einsum("qd,kd->qk", query_rows, key_rows, preferred_element_type=jnp.float32)
        * score_scale
    )
    col_pos = jnp.arange(key_rows.shape[0], dtype=jnp.int32)[None, :]
    offset = row_pos[:, None] - col_pos
    return jnp.where(offset >= 0, scores - alibi_slope * offset.astype(jnp.float32), -jnp.inf)


def attend_rows(queries, keys_values, row_pos, alibi_slope, block_rows, key_span):
    head_dim = queries.shape[1]
    score_scale = head_dim ** (-0.5)
    key_part = keys_values[:, :head_dim]
    values = keys_values[:, head_dim:]
    outputs = []
    totals = []
    for block_at in range(queries.shape[0] // block_rows):
        start_row = block_at * block_rows
        end_row = start_row + block_rows
        key_end = (block_at + 1) * key_span
        scores = masked_scores(
            queries[start_row:end_row],
            key_part[:key_end],
            row_pos[start_row:end_row],
            alibi_slope,
            score_scale,
        )
        top_score = jnp.max(scores, axis=1, keepdims=True)
        log_total = top_score[:, 0] + jnp.log(jnp.sum(jnp.exp(scores - top_score), axis=1))
        probs = jnp.exp(scores - log_total[:, None]).astype(jnp.bfloat16)
        outputs.append(
            jnp.dot(probs, values[:key_end], preferred_element_type=jnp.float32).astype(
                jnp.bfloat16
            )
        )
        totals.append(log_total)
    return (jnp.concatenate(outputs, axis=0), jnp.concatenate(totals, axis=0))


def attend_back_rows(
    queries, keys_values, head_out, log_total, grad_out, row_pos, alibi_slope, block_rows, key_span
):
    head_dim = queries.shape[1]
    score_scale = head_dim ** (-0.5)
    length_all = keys_values.shape[0]
    key_part = keys_values[:, :head_dim]
    values = keys_values[:, head_dim:]
    row_delta = jnp.sum(grad_out.astype(jnp.float32) * head_out.astype(jnp.float32), axis=1)
    d_key_total = jnp.zeros((length_all, head_dim), jnp.float32)
    d_value_total = jnp.zeros((length_all, head_dim), jnp.float32)
    d_query_rows = []
    for block_at in range(queries.shape[0] // block_rows):
        start_row = block_at * block_rows
        end_row = start_row + block_rows
        key_end = (block_at + 1) * key_span
        query_rows = queries[start_row:end_row]
        grad_rows = grad_out[start_row:end_row]
        scores = masked_scores(
            query_rows, key_part[:key_end], row_pos[start_row:end_row], alibi_slope, score_scale
        )
        probs = jnp.exp(scores - log_total[start_row:end_row, None])
        probs_low = probs.astype(jnp.bfloat16)
        d_value_total = d_value_total.at[:key_end].add(
            jnp.einsum("qk,qd->kd", probs_low, grad_rows, preferred_element_type=jnp.float32)
        )
        d_probs = jnp.einsum(
            "qd,kd->qk", grad_rows, values[:key_end], preferred_element_type=jnp.float32
        )
        d_scores = (probs * (d_probs - row_delta[start_row:end_row, None])).astype(jnp.bfloat16)
        d_query_rows.append(
            jnp.dot(d_scores, key_part[:key_end], preferred_element_type=jnp.float32) * score_scale
        )
        d_key_total = d_key_total.at[:key_end].add(
            jnp.einsum("qk,qd->kd", d_scores, query_rows, preferred_element_type=jnp.float32)
            * score_scale
        )
    d_query = jnp.concatenate(d_query_rows, axis=0)
    return (d_query, jnp.concatenate([d_key_total, d_value_total], axis=1))


def shards(
    tokens,
    qkv_weight,
    dense_weight,
    fc1_weight,
    fc2_weight,
    query_bias,
    value_bias,
    dense_bias,
    fc1_bias,
    fc2_bias,
    norm1_gain,
    norm1_shift,
    norm2_gain,
    norm2_shift,
    out_grad,
):
    rep_count, seq_rows, model_width = tokens.shape
    head_dim = model_width // HEADS
    group_size = lax.axis_size("seq")
    fsdp_size = lax.axis_size("fsdp")
    quarters = group_size // HEADS
    quarter_rows = seq_rows // quarters
    sources_per_block = min(group_size, max(1, 512 // quarter_rows))
    block_rows = sources_per_block * quarter_rows
    key_span = sources_per_block * seq_rows
    seq_place = lax.axis_index("seq")
    fsdp_place = lax.axis_index("fsdp")
    seq_bits = group_size.bit_length() - 1
    head_index = seq_place // quarters
    quarter_index = seq_place % quarters
    alibi_slope = jnp.exp2(-8.0 * (head_index + 1).astype(jnp.float32) / HEADS)
    row_index = jnp.arange(group_size * quarter_rows, dtype=jnp.int32)
    row_pos = (
        row_index // quarter_rows * seq_rows
        + quarter_index * quarter_rows
        + row_index % quarter_rows
    )

    def bit(place):
        return (seq_place >> place) & 1

    def swap_bit(array, place):
        pairs = [(at, at ^ (1 << place)) for at in range(group_size)]
        return lax.ppermute(array, "seq", pairs)

    def swap_fsdp(array):
        return lax.ppermute(array, "fsdp", [(at, at ^ 1) for at in range(fsdp_size)])

    def pick(array, index, dim):
        return lax.dynamic_index_in_dim(array, index, dim, keepdims=False)

    def xor_order(array, dim):
        array = jnp.where(bit(1) == 1, jnp.flip(array, dim), array)
        return jnp.where(bit(0) == 1, jnp.flip(array, dim + 1), array)

    def halves(own, other, dim):
        return jnp.where(
            fsdp_place == 0,
            jnp.concatenate([own, other], dim),
            jnp.concatenate([other, own], dim),
        )

    def fetch_start(own, after):
        rows, columns = own.shape
        part = pick(own.reshape(4, rows // 4, columns), bit(1) * 2 + bit(0), 0)
        if after is not None:
            part, _ = lax.optimization_barrier((part, after))
        return swap_fsdp(part)

    def fetch_rest(part):
        across = swap_bit(part, 1)
        near = swap_bit(part, 0)
        near_across = swap_bit(across, 0)
        return jnp.concatenate([part, near, across, near_across], axis=0)

    def split_columns(array):
        rows, columns = array.shape
        half = columns // 2
        own = lax.dynamic_slice_in_dim(array, fsdp_place * half, half, 1)
        other = lax.dynamic_slice_in_dim(array, (1 - fsdp_place) * half, half, 1)
        other = xor_order(other.reshape(rows, 2, 2, half // 4), 1).reshape(rows, half)
        return own, other

    def times(array, weight):
        own, other = split_columns(array)
        return jnp.dot(own, weight[0], preferred_element_type=jnp.float32) + jnp.dot(
            other, weight[1], preferred_element_type=jnp.float32
        )

    def times_turned(array, weight):
        turned = (((1,), (1,)), ((), ()))
        own = lax.dot_general(array, weight[0], turned, preferred_element_type=jnp.float32)
        other = lax.dot_general(array, weight[1], turned, preferred_element_type=jnp.float32)
        rows, half = other.shape
        other = xor_order(other.reshape(rows, 2, 2, half // 4), 1).reshape(rows, half)
        return halves(own, other, 1)

    def halving(total, order, dims, wire):
        dims = list(dims)
        for stage in order:
            dim = dims.index(stage)
            place = fsdp_place if stage == "fsdp" else bit(stage)
            sent = pick(total, 1 - place, dim).astype(wire)
            got = swap_fsdp(sent) if stage == "fsdp" else swap_bit(sent, stage)
            total = pick(total, place, dim) + got.astype(jnp.float32)
            dims.pop(dim)
        return total

    high_bits = list(range(seq_bits - 1, 0, -1))
    low_bits = list(range(2, seq_bits))
    order_one = ["fsdp", 1] + low_bits
    order_two = [1, "fsdp"] + low_bits

    def both_rows(array):
        return jnp.concatenate([array, swap_bit(array, 0)], axis=0)

    def both_columns(array):
        rows, columns = array.shape
        blocks = array.reshape(rows, group_size // 2, 2, columns // group_size)
        kept = pick(blocks, bit(0), 2).reshape(rows, columns // 2)
        sent = pick(blocks, 1 - bit(0), 2).reshape(rows, columns // 2)
        return jnp.concatenate([kept, swap_bit(sent, 0)], axis=0)

    def weight_grad(left, right, order):
        total = lax.dot_general(
            left, right, (((0,), (0,)), ((), ())), preferred_element_type=jnp.float32
        )
        rows, columns = total.shape
        block = rows // (group_size // 2) // fsdp_size
        total = total.reshape([2] * len(high_bits) + [fsdp_size, block, columns])
        return halving(total, order, high_bits + ["fsdp"], jnp.bfloat16)

    small = [
        query_bias,
        value_bias,
        dense_bias,
        fc1_bias,
        fc2_bias,
        norm1_gain,
        norm1_shift,
        norm2_gain,
        norm2_shift,
    ]
    small_own = jnp.concatenate([part[0] for part in small])
    small_other = swap_fsdp(small_own)
    small_full = []
    start_at = 0
    for part in small:
        end_at = start_at + part.shape[1]
        small_full.append(
            halves(small_own[start_at:end_at], small_other[start_at:end_at], 0).astype(jnp.float32)
        )
        start_at = end_at
    q_bias, v_bias, d_bias, up_bias, down_bias, gain_one, shift_one, gain_two, shift_two = small_full

    qkv_part = fetch_start(qkv_weight[0], None)
    dense_part = fetch_start(dense_weight[0], qkv_part)
    fc1_part = fetch_start(fc1_weight[0], dense_part)
    fc2_part = fetch_start(fc2_weight[0], fc1_part)
    w_qkv = (qkv_weight[0], fetch_rest(qkv_part))
    w_dense = (dense_weight[0], fetch_rest(dense_part))
    w_up = (fc1_weight[0], fetch_rest(fc1_part))
    w_down = (fc2_weight[0], fetch_rest(fc2_part))

    hidden = tokens[0].astype(jnp.float32)
    normed_in, hat_one, inv_one = layer_norm(hidden, gain_one, shift_one)
    attn_in = normed_in.astype(jnp.bfloat16)
    full_bias = jnp.concatenate(
        [
            q_bias.reshape(HEADS, head_dim),
            jnp.zeros((HEADS, head_dim), jnp.float32),
            v_bias.reshape(HEADS, head_dim),
        ],
        axis=1,
    ).reshape(-1)
    packed = (times(attn_in, w_qkv) + full_bias).astype(jnp.bfloat16)
    packed_heads = packed.reshape(seq_rows, HEADS, 3 * head_dim).transpose(1, 0, 2)
    if quarters == 1:
        packed_recv = lax.all_to_all(packed_heads, "seq", split_axis=0, concat_axis=0, tiled=True)
        packed_recv = packed_recv.reshape(group_size * seq_rows, 3 * head_dim)
        query_recv = packed_recv[:, :head_dim]
        pair_recv = packed_recv[:, head_dim:]
    else:
        query_send = packed_heads[:, :, :head_dim].reshape(group_size, quarter_rows, head_dim)
        pair_send = jnp.broadcast_to(
            packed_heads[:, None, :, head_dim:], (HEADS, quarters, seq_rows, 2 * head_dim)
        ).reshape(group_size, seq_rows, 2 * head_dim)
        query_recv = lax.all_to_all(query_send, "seq", split_axis=0, concat_axis=1, tiled=True)[0]
        pair_recv = lax.all_to_all(pair_send, "seq", split_axis=0, concat_axis=1, tiled=True)[0]
    head_out, log_total = attend_rows(
        query_recv, pair_recv, row_pos, alibi_slope, block_rows, key_span
    )
    arrived = lax.all_to_all(head_out[None], "seq", split_axis=1, concat_axis=0, tiled=True)
    mixed = (
        arrived.reshape(HEADS, seq_rows, head_dim).transpose(1, 0, 2).reshape(seq_rows, model_width)
    )
    after_attn = hidden + times(mixed, w_dense) + d_bias
    normed_mid, hat_two, inv_two = layer_norm(after_attn, gain_two, shift_two)
    mlp_in = normed_mid.astype(jnp.bfloat16)
    pre_act = times(mlp_in, w_up) + up_bias
    activation, gelu_slope = gelu_parts(pre_act)
    act_low = activation.astype(jnp.bfloat16)
    result = (after_attn + times(act_low, w_down) + down_bias).astype(jnp.bfloat16)

    up_low = out_grad[0]
    upstream = up_low.astype(jnp.float32)
    g_fc2_w = weight_grad(both_columns(act_low), both_rows(up_low), order_two)
    g_fc2_b = jnp.sum(upstream, axis=0)
    d_pre = times_turned(up_low, w_down) * gelu_slope
    d_pre_low = d_pre.astype(jnp.bfloat16)
    g_fc1_w = weight_grad(both_columns(mlp_in), both_rows(d_pre_low), order_one)
    g_fc1_b = jnp.sum(d_pre, axis=0)
    d_norm2 = times_turned(d_pre_low, w_up)
    g_gain2 = jnp.sum(d_norm2 * hat_two, axis=0)
    g_shift2 = jnp.sum(d_norm2, axis=0)
    d_after = upstream + norm_back(d_norm2, hat_two, inv_two, gain_two)
    d_after_low = d_after.astype(jnp.bfloat16)
    g_dense_w = weight_grad(both_columns(mixed), both_rows(d_after_low), order_two)
    g_dense_b = jnp.sum(d_after, axis=0)
    d_mixed = times_turned(d_after_low, w_dense).astype(jnp.bfloat16)
    grad_send = (
        d_mixed.reshape(seq_rows, HEADS, head_dim)
        .transpose(1, 0, 2)
        .reshape(group_size, quarter_rows, head_dim)
    )
    grad_recv = lax.all_to_all(grad_send, "seq", split_axis=0, concat_axis=1, tiled=True)[0]
    d_query, d_pair = attend_back_rows(
        query_recv,
        pair_recv,
        head_out,
        log_total,
        grad_recv,
        row_pos,
        alibi_slope,
        block_rows,
        key_span,
    )
    if quarters == 1:
        d_all = jnp.concatenate([d_query, d_pair], axis=1).astype(jnp.bfloat16)
        d_heads = lax.all_to_all(
            d_all.reshape(group_size, seq_rows, 3 * head_dim),
            "seq",
            split_axis=0,
            concat_axis=0,
            tiled=True,
        )
    else:
        back_query = lax.all_to_all(
            d_query[None].astype(jnp.bfloat16), "seq", split_axis=1, concat_axis=0, tiled=True
        )
        back_pair = lax.all_to_all(
            d_pair[None].astype(jnp.bfloat16), "seq", split_axis=1, concat_axis=0, tiled=True
        ).astype(jnp.float32)
        query_grad = back_query.reshape(HEADS, seq_rows, head_dim)
        pair_grad = jnp.sum(back_pair.reshape(HEADS, quarters, seq_rows, 2 * head_dim), axis=1)
        d_heads = jnp.concatenate([query_grad, pair_grad.astype(jnp.bfloat16)], axis=2)
    d_packed = d_heads.transpose(1, 0, 2).reshape(seq_rows, 3 * model_width)
    attn_both = both_columns(attn_in)
    packed_both = both_rows(d_packed)
    column_half = packed_both.shape[1] // 2
    g_qkv_w = jnp.concatenate(
        [
            weight_grad(attn_both, packed_both[:, :column_half], order_one),
            weight_grad(attn_both, packed_both[:, column_half:], order_two),
        ],
        axis=1,
    )
    col_sums = jnp.sum(d_packed.astype(jnp.float32), axis=0).reshape(HEADS, 3 * head_dim)
    g_query_b = col_sums[:, :head_dim].reshape(-1)
    g_value_b = col_sums[:, 2 * head_dim :].reshape(-1)
    d_norm1 = times_turned(d_packed, w_qkv)
    g_gain1 = jnp.sum(d_norm1 * hat_one, axis=0)
    g_shift1 = jnp.sum(d_norm1, axis=0)
    input_grad = (d_after + norm_back(d_norm1, hat_one, inv_one, gain_one)).astype(jnp.bfloat16)

    vectors = [
        g_query_b,
        g_value_b,
        g_dense_b,
        g_fc1_b,
        g_fc2_b,
        g_gain1,
        g_shift1,
        g_gain2,
        g_shift2,
    ]
    vector_total = jnp.concatenate(
        [vector.reshape(group_size * fsdp_size, -1) for vector in vectors], axis=1
    ).reshape([2] * seq_bits + [fsdp_size, -1])
    vector_share = halving(
        vector_total, [0] + order_one, high_bits + [0, "fsdp"], jnp.float32
    )
    shares = []
    start_at = 0
    for vector in vectors:
        end_at = start_at + vector.shape[0] // (group_size * fsdp_size)
        shares.append(vector_share[start_at:end_at])
        start_at = end_at
    return (
        result[None],
        input_grad[None],
        g_qkv_w[None],
        g_dense_w[None],
        g_fc1_w[None],
        g_fc2_w[None],
    ) + tuple(share[None] for share in shares)


def solution(mesh):
    return jax.shard_map(
        shards,
        mesh=mesh,
        in_specs=(
            P("fsdp", "seq", None),
            P(None, "fsdp", None),
            P(None, "fsdp", None),
            P(None, "fsdp", None),
            P(None, "fsdp", None),
            P(None, "fsdp"),
            P(None, "fsdp"),
            P(None, "fsdp"),
            P(None, "fsdp"),
            P(None, "fsdp"),
            P(None, "fsdp"),
            P(None, "fsdp"),
            P(None, "fsdp"),
            P(None, "fsdp"),
            P("fsdp", "seq", None),
        ),
        out_specs=(
            P("fsdp", "seq", None),
            P("fsdp", "seq", None),
            P(None, ("seq", "fsdp"), None),
            P(None, ("seq", "fsdp"), None),
            P(None, ("seq", "fsdp"), None),
            P(None, ("seq", "fsdp"), None),
            P(None, ("seq", "fsdp")),
            P(None, ("seq", "fsdp")),
            P(None, ("seq", "fsdp")),
            P(None, ("seq", "fsdp")),
            P(None, ("seq", "fsdp")),
            P(None, ("seq", "fsdp")),
            P(None, ("seq", "fsdp")),
            P(None, ("seq", "fsdp")),
            P(None, ("seq", "fsdp")),
        ),
        check_vma=False,
    )
```

```python
import jax
import jax.numpy as jnp
from jax import lax
from jax.sharding import PartitionSpec as P

HEADS = 16


NORM_EPS = 1e-05
GELU_COEF = 0.7978845608028654
GELU_CUBE = 0.044715


def layer_norm(hidden, gain, shift):
    average = jnp.mean(hidden, axis=-1, keepdims=True)
    centred = hidden - average
    inv_std = lax.rsqrt(jnp.mean(centred * centred, axis=-1, keepdims=True) + NORM_EPS)
    normed = centred * inv_std
    return (normed * gain + shift, normed, inv_std)


def norm_back(upstream, normed, inv_std, gain):
    scaled = upstream * gain
    mean_one = jnp.mean(scaled, axis=-1, keepdims=True)
    second = jnp.mean(scaled * normed, axis=-1, keepdims=True)
    return inv_std * (scaled - mean_one - normed * second)


def gelu_parts(inputs):
    cubed_in = inputs * inputs * inputs
    tangent = jnp.tanh(GELU_COEF * (inputs + GELU_CUBE * cubed_in))
    result = 0.5 * inputs * (1.0 + tangent)
    derivative = 0.5 * (1.0 + tangent) + 0.5 * inputs * (1.0 - tangent * tangent) * GELU_COEF * (
        1.0 + 3.0 * GELU_CUBE * inputs * inputs
    )
    return (result, derivative)


def masked_scores(query_rows, key_rows, row_pos, alibi_slope, score_scale):
    scores = (
        jnp.einsum("qd,kd->qk", query_rows, key_rows, preferred_element_type=jnp.float32)
        * score_scale
    )
    col_pos = jnp.arange(key_rows.shape[0], dtype=jnp.int32)[None, :]
    offset = row_pos[:, None] - col_pos
    return jnp.where(offset >= 0, scores - alibi_slope * offset.astype(jnp.float32), -jnp.inf)


def attend_rows(queries, keys_values, row_pos, alibi_slope, block_rows, key_span):
    head_dim = queries.shape[1]
    score_scale = head_dim ** (-0.5)
    key_part = keys_values[:, :head_dim]
    values = keys_values[:, head_dim:]
    outputs = []
    totals = []
    for block_at in range(queries.shape[0] // block_rows):
        start_row = block_at * block_rows
        end_row = start_row + block_rows
        key_end = (block_at + 1) * key_span
        scores = masked_scores(
            queries[start_row:end_row],
            key_part[:key_end],
            row_pos[start_row:end_row],
            alibi_slope,
            score_scale,
        )
        top_score = jnp.max(scores, axis=1, keepdims=True)
        log_total = top_score[:, 0] + jnp.log(jnp.sum(jnp.exp(scores - top_score), axis=1))
        probs = jnp.exp(scores - log_total[:, None]).astype(jnp.bfloat16)
        outputs.append(
            jnp.dot(probs, values[:key_end], preferred_element_type=jnp.float32).astype(
                jnp.bfloat16
            )
        )
        totals.append(log_total)
    return (jnp.concatenate(outputs, axis=0), jnp.concatenate(totals, axis=0))


def attend_back_rows(
    queries, keys_values, head_out, log_total, grad_out, row_pos, alibi_slope, block_rows, key_span
):
    head_dim = queries.shape[1]
    score_scale = head_dim ** (-0.5)
    length_all = keys_values.shape[0]
    key_part = keys_values[:, :head_dim]
    values = keys_values[:, head_dim:]
    row_delta = jnp.sum(grad_out.astype(jnp.float32) * head_out.astype(jnp.float32), axis=1)
    d_key_total = jnp.zeros((length_all, head_dim), jnp.float32)
    d_value_total = jnp.zeros((length_all, head_dim), jnp.float32)
    d_query_rows = []
    for block_at in range(queries.shape[0] // block_rows):
        start_row = block_at * block_rows
        end_row = start_row + block_rows
        key_end = (block_at + 1) * key_span
        query_rows = queries[start_row:end_row]
        grad_rows = grad_out[start_row:end_row]
        scores = masked_scores(
            query_rows, key_part[:key_end], row_pos[start_row:end_row], alibi_slope, score_scale
        )
        probs = jnp.exp(scores - log_total[start_row:end_row, None])
        probs_low = probs.astype(jnp.bfloat16)
        d_value_total = d_value_total.at[:key_end].add(
            jnp.einsum("qk,qd->kd", probs_low, grad_rows, preferred_element_type=jnp.float32)
        )
        d_probs = jnp.einsum(
            "qd,kd->qk", grad_rows, values[:key_end], preferred_element_type=jnp.float32
        )
        d_scores = (probs * (d_probs - row_delta[start_row:end_row, None])).astype(jnp.bfloat16)
        d_query_rows.append(
            jnp.dot(d_scores, key_part[:key_end], preferred_element_type=jnp.float32) * score_scale
        )
        d_key_total = d_key_total.at[:key_end].add(
            jnp.einsum("qk,qd->kd", d_scores, query_rows, preferred_element_type=jnp.float32)
            * score_scale
        )
    d_query = jnp.concatenate(d_query_rows, axis=0)
    return (d_query, jnp.concatenate([d_key_total, d_value_total], axis=1))


def shards(
    tokens,
    qkv_weight,
    dense_weight,
    fc1_weight,
    fc2_weight,
    query_bias,
    value_bias,
    dense_bias,
    fc1_bias,
    fc2_bias,
    norm1_gain,
    norm1_shift,
    norm2_gain,
    norm2_shift,
    out_grad,
):
    rep_count, seq_rows, model_width = tokens.shape
    head_dim = model_width // HEADS
    group_size = lax.axis_size("seq")
    fsdp_size = lax.axis_size("fsdp")
    quarters = group_size // HEADS
    quarter_rows = seq_rows // quarters
    sources_per_block = min(group_size, max(1, 512 // quarter_rows))
    block_rows = sources_per_block * quarter_rows
    key_span = sources_per_block * seq_rows
    seq_place = lax.axis_index("seq")
    fsdp_place = lax.axis_index("fsdp")
    seq_bits = group_size.bit_length() - 1
    head_index = seq_place // quarters
    quarter_index = seq_place % quarters
    alibi_slope = jnp.exp2(-8.0 * (head_index + 1).astype(jnp.float32) / HEADS)
    row_index = jnp.arange(group_size * quarter_rows, dtype=jnp.int32)
    row_pos = (
        row_index // quarter_rows * seq_rows
        + quarter_index * quarter_rows
        + row_index % quarter_rows
    )

    def bit(place):
        return (seq_place >> place) & 1

    def swap_bit(array, place):
        pairs = [(at, at ^ (1 << place)) for at in range(group_size)]
        return lax.ppermute(array, "seq", pairs)

    def swap_fsdp(array):
        return lax.ppermute(array, "fsdp", [(at, at ^ 1) for at in range(fsdp_size)])

    def pick(array, index, dim):
        return lax.dynamic_index_in_dim(array, index, dim, keepdims=False)

    def halves(own, other, dim):
        first = fsdp_place == 0
        return jnp.concatenate([jnp.where(first, own, other), jnp.where(first, other, own)], dim)

    def tied(array, *after):
        return lax.optimization_barrier((array,) + after)[0]

    def fetch_start(own):
        rows, columns = own.shape
        return pick(own.reshape(4, rows // 4, columns), bit(1) * 2 + bit(0), 0)

    def fetch_rest(part, across):
        near = swap_bit(part, 0)
        near_across = swap_bit(across, 0)
        rows, columns = part.shape
        other = jnp.zeros((4 * rows, columns), part.dtype)
        own_place = bit(1) * 2 + bit(0)
        for flip, piece in enumerate((part, near, across, near_across)):
            other = lax.dynamic_update_slice_in_dim(other, piece, (own_place ^ flip) * rows, 0)
        return other, near_across

    def split_columns(array):
        half = array.shape[1] // 2
        own = lax.dynamic_slice_in_dim(array, fsdp_place * half, half, 1)
        other = lax.dynamic_slice_in_dim(array, (1 - fsdp_place) * half, half, 1)
        return own, other

    def times(array, weight):
        own, other = split_columns(array)
        return jnp.dot(own, weight[0], preferred_element_type=jnp.float32) + jnp.dot(
            other, weight[1], preferred_element_type=jnp.float32
        )

    def times_turned(array, weight):
        turned = (((1,), (1,)), ((), ()))
        own = lax.dot_general(array, weight[0], turned, preferred_element_type=jnp.float32)
        other = lax.dot_general(array, weight[1], turned, preferred_element_type=jnp.float32)
        return halves(own, other, 1)

    def halving_start(total, stage, dims, wire):
        dim = dims.index(stage)
        place = fsdp_place if stage == "fsdp" else bit(stage)
        sent = pick(total, 1 - place, dim).astype(wire)
        got = swap_fsdp(sent) if stage == "fsdp" else swap_bit(sent, stage)
        return pick(total, place, dim), sent, got

    def halving_rest(kept, got, order, dims, wire):
        dims = list(dims)
        dims.remove(order[0])
        total = kept + got.astype(jnp.float32)
        for stage in order[1:]:
            kept, _, got = halving_start(total, stage, dims, wire)
            total = kept + got.astype(jnp.float32)
            dims.remove(stage)
        return total

    high_bits = list(range(seq_bits - 1, 0, -1))
    low_bits = list(range(2, seq_bits))
    order_one = ["fsdp", 1] + low_bits
    order_two = [1, "fsdp"] + low_bits

    grad_dims = high_bits + ["fsdp"]

    def both_rows(array):
        return jnp.concatenate([array, swap_bit(array, 0)], axis=0)

    def both_columns(array):
        rows, columns = array.shape
        width = columns // group_size
        if width % 128 == 0:
            odd = bit(0) == 1
            parts = [array[:, at : at + width] for at in range(0, columns, width)]
            pairs = list(zip(parts[::2], parts[1::2]))
            kept = jnp.concatenate([jnp.where(odd, b, a) for a, b in pairs], axis=1)
            sent = jnp.concatenate([jnp.where(odd, a, b) for a, b in pairs], axis=1)
            return jnp.concatenate([kept, swap_bit(sent, 0)], axis=0)
        blocks = array.reshape(rows, group_size // 2, 2, columns // group_size)
        kept = pick(blocks, bit(0), 2).reshape(rows, columns // 2)
        sent = pick(blocks, 1 - bit(0), 2).reshape(rows, columns // 2)
        return jnp.concatenate([kept, swap_bit(sent, 0)], axis=0)

    def weight_grad(left, right, order):
        total = lax.dot_general(
            left, right, (((0,), (0,)), ((), ())), preferred_element_type=jnp.float32
        )
        rows, columns = total.shape
        block = rows // (group_size // 2) // fsdp_size
        total = total.reshape([2] * len(high_bits) + [fsdp_size, block, columns])
        kept, sent, got = halving_start(total, order[0], grad_dims, jnp.bfloat16)
        return kept, sent, got, order

    def grad_next(started):
        kept, _, got, order = started
        total = kept + got.astype(jnp.float32)
        dims = [dim for dim in grad_dims if dim != order[0]]
        return halving_start(total, order[1], dims, jnp.bfloat16) + (order,)

    def grad_rest(started, skip=0, after=None):
        kept, _, got, order = started
        if after is not None:
            got = tied(got, after)
        dims = [dim for dim in grad_dims if dim not in order[:skip]]
        return halving_rest(kept, got, order[skip:], dims, jnp.bfloat16)

    small = [
        query_bias,
        value_bias,
        dense_bias,
        fc1_bias,
        fc2_bias,
        norm1_gain,
        norm1_shift,
        norm2_gain,
        norm2_shift,
    ]
    small_own = jnp.concatenate(small, axis=1)
    small_other = swap_fsdp(small_own)
    small_first = jnp.where(fsdp_place == 0, small_own, small_other).astype(jnp.float32)
    small_second = jnp.where(fsdp_place == 0, small_other, small_own).astype(jnp.float32)
    small_full = []
    start_at = 0
    for part in small:
        end_at = start_at + part.shape[1]
        small_full.append(
            jnp.concatenate(
                [small_first[:, start_at:end_at], small_second[:, start_at:end_at]], axis=1
            )
        )
        start_at = end_at
    q_bias, v_bias, d_bias, up_bias, down_bias, gain_one, shift_one, gain_two, shift_two = small_full

    qkv_part = swap_fsdp(fetch_start(qkv_weight[0]))
    qkv_across = swap_bit(qkv_part, 1)
    qkv_other, qkv_last = fetch_rest(qkv_part, qkv_across)
    dense_part = swap_fsdp(tied(fetch_start(dense_weight[0]), qkv_part))
    dense_part = tied(dense_part, qkv_across)
    dense_across = swap_bit(dense_part, 1)
    dense_other, _ = fetch_rest(dense_part, dense_across)
    fc1_part = swap_fsdp(tied(fetch_start(fc1_weight[0]), qkv_part))
    fc1_part = tied(fc1_part, qkv_last)
    fc1_across = swap_bit(fc1_part, 1)
    fc1_other, _ = fetch_rest(fc1_part, fc1_across)
    fc2_part = swap_fsdp(tied(fetch_start(fc2_weight[0]), qkv_across))
    fc2_part = tied(fc2_part, qkv_last)
    fc2_across = swap_bit(fc2_part, 1)
    fc2_other, _ = fetch_rest(fc2_part, fc2_across)
    w_qkv = (qkv_weight[0], qkv_other)
    w_dense = (dense_weight[0], dense_other)
    w_up = (fc1_weight[0], fc1_other)
    w_down = (fc2_weight[0], fc2_other)

    hidden = tokens[0].astype(jnp.float32)
    normed_in, hat_one, inv_one = layer_norm(hidden, gain_one, shift_one)
    attn_in = normed_in.astype(jnp.bfloat16)
    full_bias = jnp.concatenate(
        [
            q_bias.reshape(HEADS, head_dim),
            jnp.zeros((HEADS, head_dim), jnp.float32),
            v_bias.reshape(HEADS, head_dim),
        ],
        axis=1,
    ).reshape(1, -1)
    packed = (times(attn_in, w_qkv) + full_bias).astype(jnp.bfloat16)
    packed_heads = packed.reshape(seq_rows, HEADS, 3 * head_dim).transpose(1, 0, 2)
    if quarters == 1:
        packed_recv = lax.all_to_all(packed_heads, "seq", split_axis=0, concat_axis=0, tiled=True)
        packed_recv = packed_recv.reshape(group_size * seq_rows, 3 * head_dim)
        query_recv = packed_recv[:, :head_dim]
        pair_recv = packed_recv[:, head_dim:]
    else:
        query_send = packed_heads[:, :, :head_dim].reshape(group_size, quarter_rows, head_dim)
        pair_send = jnp.broadcast_to(
            packed_heads[:, None, :, head_dim:], (HEADS, quarters, seq_rows, 2 * head_dim)
        ).reshape(group_size, seq_rows, 2 * head_dim)
        query_recv = lax.all_to_all(query_send, "seq", split_axis=0, concat_axis=1, tiled=True)[0]
        pair_recv = lax.all_to_all(pair_send, "seq", split_axis=0, concat_axis=1, tiled=True)[0]
    head_out, log_total = attend_rows(
        query_recv, pair_recv, row_pos, alibi_slope, block_rows, key_span
    )
    arrived = lax.all_to_all(
        head_out.reshape(group_size, quarter_rows, head_dim),
        "seq",
        split_axis=0,
        concat_axis=0,
        tiled=True,
    )
    mixed = (
        arrived.reshape(HEADS, seq_rows, head_dim).transpose(1, 0, 2).reshape(seq_rows, model_width)
    )
    after_attn = hidden + times(mixed, w_dense) + d_bias
    normed_mid, hat_two, inv_two = layer_norm(after_attn, gain_two, shift_two)
    mlp_in = normed_mid.astype(jnp.bfloat16)
    pre_act = times(mlp_in, w_up) + up_bias
    activation, gelu_slope = gelu_parts(pre_act)
    act_low = activation.astype(jnp.bfloat16)
    result = (after_attn + times(act_low, w_down) + down_bias).astype(jnp.bfloat16)

    up_low = out_grad[0]
    upstream = up_low.astype(jnp.float32)
    s_fc2 = weight_grad(both_columns(act_low), both_rows(up_low), order_two)
    g_fc2_b = jnp.sum(upstream, axis=0)
    d_pre = times_turned(up_low, w_down) * gelu_slope
    d_pre_low = d_pre.astype(jnp.bfloat16)
    s_fc1 = weight_grad(both_columns(mlp_in), both_rows(d_pre_low), order_one)
    g_fc1_b = jnp.sum(d_pre, axis=0)
    d_norm2 = times_turned(d_pre_low, w_up)
    g_gain2 = jnp.sum(d_norm2 * hat_two, axis=0)
    g_shift2 = jnp.sum(d_norm2, axis=0)
    d_after = upstream + norm_back(d_norm2, hat_two, inv_two, gain_two)
    d_after_low = d_after.astype(jnp.bfloat16)
    s_dense = weight_grad(both_columns(mixed), both_rows(d_after_low), order_two)
    g_dense_b = jnp.sum(d_after, axis=0)
    d_mixed = times_turned(d_after_low, w_dense).astype(jnp.bfloat16)
    d_mixed = tied(d_mixed, s_fc2[1], s_fc1[1])
    grad_send = (
        d_mixed.reshape(seq_rows, HEADS, head_dim)
        .transpose(1, 0, 2)
        .reshape(group_size, quarter_rows, head_dim)
    )
    grad_recv = lax.all_to_all(grad_send, "seq", split_axis=0, concat_axis=0, tiled=True)
    grad_recv = grad_recv.reshape(group_size * quarter_rows, head_dim)
    n_fc2 = grad_next(s_fc2)
    grad_recv = tied(grad_recv, n_fc2[1], s_dense[1])
    d_query, d_pair = attend_back_rows(
        query_recv,
        pair_recv,
        head_out,
        log_total,
        grad_recv,
        row_pos,
        alibi_slope,
        block_rows,
        key_span,
    )
    n_fc1 = grad_next(s_fc1)
    d_query = tied(d_query, n_fc1[1])
    if quarters == 1:
        d_all = jnp.concatenate([d_query, d_pair], axis=1).astype(jnp.bfloat16)
        d_heads = lax.all_to_all(
            d_all.reshape(group_size, seq_rows, 3 * head_dim),
            "seq",
            split_axis=0,
            concat_axis=0,
            tiled=True,
        )
    else:
        back_query = lax.all_to_all(
            d_query.astype(jnp.bfloat16).reshape(group_size, quarter_rows, head_dim),
            "seq",
            split_axis=0,
            concat_axis=0,
            tiled=True,
        )
        back_pair = lax.all_to_all(
            d_pair.astype(jnp.bfloat16).reshape(group_size, seq_rows, 2 * head_dim),
            "seq",
            split_axis=0,
            concat_axis=0,
            tiled=True,
        ).astype(jnp.float32)
        query_grad = back_query.reshape(HEADS, seq_rows, head_dim)
        pair_grad = jnp.sum(back_pair.reshape(HEADS, quarters, seq_rows, 2 * head_dim), axis=1)
        d_heads = jnp.concatenate([query_grad, pair_grad.astype(jnp.bfloat16)], axis=2)
    d_packed = d_heads.transpose(1, 0, 2).reshape(seq_rows, 3 * model_width)
    attn_both = both_columns(attn_in)
    packed_both = both_rows(d_packed)
    column_half = packed_both.shape[1] // 2
    s_qkv_one = weight_grad(attn_both, packed_both[:, :column_half], order_one)
    s_qkv_two = weight_grad(attn_both, packed_both[:, column_half:], order_two)
    g_fc2_w = grad_rest(n_fc2, 1, d_heads)
    g_fc1_w = grad_rest(n_fc1, 1, d_heads)
    g_dense_w = grad_rest(s_dense, 0, d_heads)
    g_qkv_w = jnp.concatenate([grad_rest(s_qkv_one), grad_rest(s_qkv_two)], axis=1)
    col_sums = jnp.sum(d_packed.astype(jnp.float32), axis=0).reshape(HEADS, 3 * head_dim)
    g_query_b = col_sums[:, :head_dim].reshape(-1)
    g_value_b = col_sums[:, 2 * head_dim :].reshape(-1)
    d_norm1 = times_turned(d_packed, w_qkv)
    g_gain1 = jnp.sum(d_norm1 * hat_one, axis=0)
    g_shift1 = jnp.sum(d_norm1, axis=0)
    input_grad = (d_after + norm_back(d_norm1, hat_one, inv_one, gain_one)).astype(jnp.bfloat16)

    vectors = [
        g_query_b,
        g_value_b,
        g_dense_b,
        g_fc1_b,
        g_fc2_b,
        g_gain1,
        g_shift1,
        g_gain2,
        g_shift2,
    ]
    vector_total = jnp.concatenate(
        [vector.reshape(group_size * fsdp_size, -1) for vector in vectors], axis=1
    ).reshape([2] * seq_bits + [fsdp_size, -1])
    vector_total = tied(vector_total, s_qkv_one[1], s_qkv_two[1])
    vector_dims = high_bits + [0, "fsdp"]
    vector_order = low_bits + [0] + [1, "fsdp"]
    kept, _, got = halving_start(vector_total, vector_order[0], vector_dims, jnp.float32)
    vector_share = halving_rest(kept, got, vector_order, vector_dims, jnp.float32)
    shares = []
    start_at = 0
    for vector in vectors:
        end_at = start_at + vector.shape[0] // (group_size * fsdp_size)
        shares.append(vector_share[start_at:end_at])
        start_at = end_at
    return (
        result[None],
        input_grad[None],
        g_qkv_w[None],
        g_dense_w[None],
        g_fc1_w[None],
        g_fc2_w[None],
    ) + tuple(share[None] for share in shares)


def solution(mesh):
    return jax.shard_map(
        shards,
        mesh=mesh,
        in_specs=(
            P("fsdp", "seq", None),
            P(None, "fsdp", None),
            P(None, "fsdp", None),
            P(None, "fsdp", None),
            P(None, "fsdp", None),
            P(None, "fsdp"),
            P(None, "fsdp"),
            P(None, "fsdp"),
            P(None, "fsdp"),
            P(None, "fsdp"),
            P(None, "fsdp"),
            P(None, "fsdp"),
            P(None, "fsdp"),
            P(None, "fsdp"),
            P("fsdp", "seq", None),
        ),
        out_specs=(
            P("fsdp", "seq", None),
            P("fsdp", "seq", None),
            P(None, ("seq", "fsdp"), None),
            P(None, ("seq", "fsdp"), None),
            P(None, ("seq", "fsdp"), None),
            P(None, ("seq", "fsdp"), None),
            P(None, ("seq", "fsdp")),
            P(None, ("seq", "fsdp")),
            P(None, ("seq", "fsdp")),
            P(None, ("seq", "fsdp")),
            P(None, ("seq", "fsdp")),
            P(None, ("seq", "fsdp")),
            P(None, ("seq", "fsdp")),
            P(None, ("seq", "fsdp")),
            P(None, ("seq", "fsdp")),
        ),
        check_vma=False,
    )
```
